32 devices in a mesh: depth: 4 (over z), imx: 4 (over y, x), imy: 2 (over core).
Axes of the slice: x: 2, y: 2, z: 4, core: 2. Of those that a mesh axis runs over, the one named last changes fastest.
Arguments:
- field: bfloat16 [128, 256, 512], P('depth', 'imy', 'imx'), may hold values from -6 to 6
- brick_live: int32 [4, 8, 16], P('depth', 'imy', 'imx'), may hold values from 0 to 1, as said below
- order: int32 [32, 64], P('imy', 'imx'), may hold values 0 or 1
- centers: float32 [4], replicated, may hold values from -2 to 2
- widths: float32 [4], replicated, may hold values from 0.3 to 1.2
- heights: float32 [4], replicated, may hold values from 0.5 to 3
- colours: float32 [4, 3], replicated, may hold values from 0.1 to 1
Outputs:
- colour: float32 [3, 256, 512], P(None, ('imy', 'depth'), 'imx')
- logtrans: float32 [256, 512], P(('imy', 'depth'), 'imx')
The draws below stay inside these ranges and needn't reach their ends.
Inputs may be any that keep to these rules, and one draw needn't show every extreme that they name: `brick_live`: each device's 16 bricks (one slab, 4 bricks along the rows by 4 along the columns) hold between 1 and 16 live bricks; at least one device has all 16 live, and most have few.
All inputs are finite; a program needn't handle non-finite values. No bound on the sum of `order` on one device may be relied on, other than what follows from the above.
Results may differ from the reference program's by a relative error of at most 0.00038.
Values may be sent and summed in bfloat16 or wider, within the bound.
A program may use at most 64 MiB of HBM per device.

```python
import math
import jax
import jax.numpy as jnp
from jax import lax

BRICK = 32
BX_DEV = 4
BY_DEV = 4
NB = 4
TILE = 8
Z_DEV = 32
BRICKS_DEV = 16
NZ = 128
NX = 256
NY = 512
SLABS = 4
ROW_BLOCKS = 2
COL_BLOCKS = 4


def draw_brick_live(key, part):
    keys = jax.random.split(jax.random.fold_in(key, 7177), 4)
    first = jax.random.randint(keys[0], (SLABS, ROW_BLOCKS, COL_BLOCKS), 0, 8)
    second = jax.random.randint(keys[1], (SLABS, ROW_BLOCKS, COL_BLOCKS), 0, 8)
    counts = 1 + first * second * (BRICKS_DEV - 1) // 49
    chosen = jax.random.randint(keys[2], (), 0, SLABS * ROW_BLOCKS * COL_BLOCKS)
    flat = jnp.arange(SLABS * ROW_BLOCKS * COL_BLOCKS, dtype=jnp.int32).reshape(SLABS, ROW_BLOCKS, COL_BLOCKS)
    counts = jnp.where(flat == chosen, BRICKS_DEV, counts)
    scores = jax.random.randint(keys[3], (SLABS, ROW_BLOCKS, COL_BLOCKS, BRICKS_DEV), 0, 1 << 20) * BRICKS_DEV
    scores = scores + jnp.arange(BRICKS_DEV, dtype=jnp.int32)[None, None, None, :]
    ranks = jnp.argsort(jnp.argsort(scores, axis=3, stable=True), axis=3, stable=True)
    live = (ranks < counts[:, :, :, None]).astype(jnp.int32)
    live = live.reshape(SLABS, ROW_BLOCKS, COL_BLOCKS, BX_DEV, BY_DEV)
    live = jnp.transpose(live, (0, 1, 3, 2, 4))
    return live.reshape(SLABS, ROW_BLOCKS * BX_DEV, COL_BLOCKS * BY_DEV)


def with_ends(entries, key, least, largest):
    dims = entries.shape
    index_at = [jax.random.randint(jax.random.fold_in(key, axis), (), 0, dims[axis]) for axis in range(len(dims))]
    entries = entries.at[tuple(index_at)].set(least)
    longest = dims.index(max(dims))
    index_at[longest] = (index_at[longest] + 1) % dims[longest]
    return entries.at[tuple(index_at)].set(largest)


def shard_levels(key, shape, shards, low, high):
    def one(axis_at, blocks):
        draws = jax.random.uniform(jax.random.fold_in(jax.random.fold_in(key, 6), axis_at), (blocks,), jnp.float32, low / len(shards), high / len(shards))
        return jnp.repeat(jnp.exp(draws), shape[axis_at] // blocks).reshape((-1,) + (1,) * (len(shape) - axis_at - 1))

    factor_of = one(*shards[0])
    for cut in shards[1:]:
        factor_of = factor_of * one(*cut)
    return factor_of


def noise(own_key, extent, width, bound, pieces=(), kind=jnp.bfloat16):
    loudness = shard_levels(own_key, extent, pieces, -0.22, 0.18) if pieces else 1.0
    drawn = jax.random.normal(own_key, extent, jnp.float32) * width * loudness
    return jnp.minimum(jnp.maximum(drawn, -bound), bound).astype(kind)


def setup_inputs(seed: int = 0) -> dict:
    seeds = jax.random.split(jax.random.key(seed), 8)
    return {
        "field": noise(seeds[0], (NZ, NX, NY), 1.0, 6.0, ((0, 4), (1, 2), (2, 4))),
        "brick_live": draw_brick_live(jax.random.fold_in(seeds[7], 71), 0),
        "order": with_ends((jax.random.randint(seeds[2], (NX // TILE, NY // TILE), 0, 2) < 1).astype(jnp.int32), jax.random.fold_in(seeds[2], 1), 0, 1),
        "centers": jnp.clip(jax.random.uniform(seeds[3], (NB,), jnp.float32, -2.0, 2.0), -2.0, 2.0),
        "widths": jnp.clip(jnp.exp(jax.random.uniform(seeds[4], (NB,), jnp.float32, math.log(0.3), math.log(1.2))), 0.3, 1.2),
        "heights": jnp.clip(jnp.exp(jax.random.uniform(seeds[5], (NB,), jnp.float32, math.log(0.5), math.log(3.0))), 0.5, 3.0),
        "colours": jnp.clip(jax.random.uniform(seeds[6], (NB, 3), jnp.float32, 0.1, 1.0), 0.1, 1.0),
    }


OPTICAL = 3.0

def shade_cells(padded):
    grad_z = (padded[2:, 1:-1, 1:-1] - padded[:-2, 1:-1, 1:-1]) * 0.5
    grad_x = (padded[1:-1, 2:, 1:-1] - padded[1:-1, :-2, 1:-1]) * 0.5
    grad_y = (padded[1:-1, 1:-1, 2:] - padded[1:-1, 1:-1, :-2]) * 0.5
    facing = grad_z * 0.64 + grad_x * 0.48 + grad_y * 0.6
    length = lax.rsqrt(grad_z * grad_z + grad_x * grad_x + grad_y * grad_y + 1.0)
    return (0.3 + 0.7 * jnp.abs(facing) * length).astype(jnp.bfloat16)

def render_cells(values, shade, backward, live, centers, widths, heights, colours, step_len):
    valf = values.astype(jnp.float32)
    sigma = jnp.zeros(valf.shape, jnp.float32)
    emits = [jnp.zeros(valf.shape, jnp.float32) for chan in range(3)]
    for bumpno in range(centers.shape[0]):
        bump = jnp.exp(-0.5 * jnp.square((valf - centers[bumpno]) / widths[bumpno]))
        sigma = sigma + heights[bumpno] * bump
        emits = [emits[chan] + colours[bumpno, chan] * bump for chan in range(3)]
    tau = sigma * (step_len * live)
    absorb = -jnp.expm1(-tau)
    running = jnp.cumsum(tau, axis=0)
    total = running[-1]
    before = jnp.where(backward, total - running, running - tau)
    weight = jnp.exp(-before) * absorb * shade.astype(jnp.float32)
    parts = [lax.optimization_barrier(jnp.sum(weight * emits[chan], axis=0)) for chan in range(3)]
    return jnp.stack(parts + [-total])

def reference(field, brick_live, order, centers, widths, heights, colours):
    step_len = OPTICAL / NZ
    padded = jnp.pad(field, 1)
    backward = jnp.repeat(jnp.repeat(order, TILE, axis=0), TILE, axis=1) == 1

    def one_slab(slab):
        block = lax.dynamic_slice(padded, (slab * Z_DEV, jnp.int32(0), jnp.int32(0)), (Z_DEV + 2, NX + 2, NY + 2)).astype(jnp.float32)
        shade = shade_cells(block)
        live_here = lax.dynamic_index_in_dim(brick_live, slab, 0, keepdims=False)
        live = jnp.repeat(jnp.repeat(live_here, BRICK, axis=0), BRICK, axis=1).astype(jnp.float32)
        return render_cells(block[1:-1, 1:-1, 1:-1], shade, backward, live, centers, widths, heights, colours, step_len)
    tiles = lax.map(one_slab, jnp.arange(SLABS, dtype=jnp.int32))

    def over(carry, tile):
        colour_acc, logt_acc = carry
        return ((colour_acc + jnp.exp(logt_acc) * tile[:3], logt_acc + tile[3]), None)
    start = (jnp.zeros((3, NX, NY), jnp.float32), jnp.zeros((NX, NY), jnp.float32))
    forward, unused = lax.scan(over, start, tiles)
    reverse_pass, unused = lax.scan(over, start, tiles, reverse=True)
    colour = jnp.where(backward, reverse_pass[0], forward[0])
    logtrans = jnp.where(backward, reverse_pass[1], forward[1])
    return (colour, logtrans)
```

```python
import functools
import math

import jax
import jax.numpy as jnp
from jax import lax
from jax.experimental import pallas as pl
from jax.experimental.pallas import tpu as pltpu
from jax.sharding import PartitionSpec as P

OPTICAL = 3.0
MESH = pl.DeviceIdType.MESH
SUB = 8
PACK = 16
LANES = 128
F32 = jnp.float32
BF16 = jnp.bfloat16
LOG2E = math.log2(math.e)


def iota(shape, dim):
    return lax.broadcasted_iota(jnp.int32, shape, dim)


def expand(small, rows, cols):
    high, wide = small.shape
    down = (iota((rows, high), 0) // (rows // high) == iota((rows, high), 1)).astype(F32).astype(BF16)
    along = (iota((wide, cols), 1) // (cols // wide) == iota((wide, cols), 0)).astype(F32).astype(BF16)
    tall = jnp.dot(down, small.astype(F32).astype(BF16), preferred_element_type=F32)
    return jnp.dot(tall.astype(BF16), along, preferred_element_type=F32)


def kernel(
    counts, step_len,
    field, live, order, centers, widths, heights, colours,
    colour_out, logt_out,
    fb, vf, zlo, zhi, xlo, xhi, face, flo, fhi, gy, factor, flag, tiles_out, tiles_in,
    field_sem, halo_send, halo_recv, tile_send, tile_recv,
):
    ndepth, nimx, nimy = counts
    me = lax.axis_index("depth")
    mx = lax.axis_index("imx")
    my = lax.axis_index("imy")
    zdev, xdev, ydev = fb.shape
    rows_out = xdev // ndepth
    nb = centers.shape[0]
    rows_blk = min(PACK, rows_out)

    load = pltpu.make_async_copy(field, fb, field_sem)
    load.start()

    barrier = pltpu.get_barrier_semaphore()
    for step in range(1, ndepth):
        pl.semaphore_signal(barrier, inc=1, device_id={"depth": lax.rem(me + step, ndepth)}, device_id_type=MESH)
    for axis, pos, count in (("imx", mx, nimx), ("imy", my, nimy)):
        @pl.when(pos > 0)
        def _():
            pl.semaphore_signal(barrier, inc=1, device_id={axis: pos - 1}, device_id_type=MESH)

        @pl.when(pos < count - 1)
        def _():
            pl.semaphore_signal(barrier, inc=1, device_id={axis: pos + 1}, device_id_type=MESH)

    back = expand(order[...], xdev, ydev)
    flag[...] = back
    factor[...] = (2.0 * back - 1.0) * expand(live[0], xdev, ydev) * (step_len * LOG2E)

    for pos, count, low, high in ((me, ndepth, zlo, zhi), (mx, nimx, flo, fhi), (my, nimy, xlo, xhi)):
        @pl.when(pos == 0)
        def _():
            low[...] = jnp.zeros_like(low)

        @pl.when(pos == count - 1)
        def _():
            high[...] = jnp.zeros_like(high)

    peers = ndepth - 1
    for pos, count in ((mx, nimx), (my, nimy)):
        peers = peers + (pos + count - 1) // count + (2 * count - 2 - pos) // count
    pl.semaphore_wait(barrier, peers)
    load.wait()

    def links(axis, pos, count, down_src, up_src, low, high, at):
        to_low = pltpu.make_async_remote_copy(
            src_ref=down_src, dst_ref=high, send_sem=halo_send.at[at], recv_sem=halo_recv.at[at],
            device_id={axis: lax.rem(pos + count - 1, count)}, device_id_type=MESH)
        to_high = pltpu.make_async_remote_copy(
            src_ref=up_src, dst_ref=low, send_sem=halo_send.at[at + 1], recv_sem=halo_recv.at[at + 1],
            device_id={axis: lax.rem(pos + 1, count)}, device_id_type=MESH)
        return pos, count, to_low, to_high

    def start(link):
        pos, count, to_low, to_high = link

        @pl.when(pos > 0)
        def _():
            to_low.start()

        @pl.when(pos < count - 1)
        def _():
            to_high.start()

    def finish(link):
        pos, count, to_low, to_high = link

        @pl.when(pos > 0)
        def _():
            to_low.wait_send()
            to_high.wait_recv()

        @pl.when(pos < count - 1)
        def _():
            to_high.wait_send()
            to_low.wait_recv()

    zlink = links("depth", me, ndepth, fb.at[0], fb.at[zdev - 1], zlo, zhi, 0)
    xlink = links("imy", my, nimy, fb.at[:, pl.ds(0, PACK)], fb.at[:, pl.ds(xdev - PACK, PACK)], xlo, xhi, 2)
    ylink = links("imx", mx, nimx, face, face, flo, fhi, 4)
    start(zlink)
    start(xlink)

    k_at, l_at = iota((ydev, LANES), 0), iota((ydev, LANES), 1)
    pick = ((k_at == 0) & (l_at < zdev)) | ((k_at == ydev - 1) & (l_at >= zdev) & (l_at < 2 * zdev))
    pick = pick.astype(F32).astype(BF16)
    lane = iota((xdev, LANES), 1)

    def pack(z, acc):
        ends = jnp.dot(fb[z], pick, preferred_element_type=F32)
        return jnp.where((lane == z) | (lane == z + zdev), ends, acc)

    packed = lax.fori_loop(0, zdev, pack, jnp.zeros((xdev, LANES), F32), unroll=4)
    face[...] = packed.astype(BF16)
    start(ylink)

    def widen(z, carry):
        vf[z + 1, SUB:SUB + xdev] = fb[z].astype(F32)
        return carry

    lax.fori_loop(0, zdev, widen, 0, unroll=4)

    finish(zlink)
    vf[0, SUB:SUB + xdev] = zlo[...].astype(F32)
    vf[zdev + 1, SUB:SUB + xdev] = zhi[...].astype(F32)
    finish(xlink)

    def widen_rows(z, carry):
        vf[z + 1, 0:SUB] = xlo[z].astype(F32)[PACK - SUB:]
        vf[z + 1, SUB + xdev:] = xhi[z].astype(F32)[:SUB]
        return carry

    lax.fori_loop(0, zdev, widen_rows, 0, unroll=4)
    finish(ylink)

    edges = jnp.where(lane < zdev, fhi[...].astype(F32), flo[...].astype(F32))
    k_at, l_at = iota((ydev + LANES, ydev), 0), iota((ydev + LANES, ydev), 1)
    plus = (k_at == l_at + 1) & (k_at < ydev) | (k_at >= ydev) & (k_at < ydev + zdev) & (l_at == ydev - 1)
    minus = (k_at == l_at - 1) | (k_at >= ydev + zdev) & (k_at < ydev + 2 * zdev) & (l_at == 0)
    slope = (plus.astype(F32) - minus.astype(F32)).astype(BF16)

    def across(z, carry):
        side = jnp.where((lane == z) | (lane == z + zdev), edges, 0.0).astype(BF16)
        gy[z] = jnp.dot(jnp.concatenate([fb[z], side], axis=1), slope, preferred_element_type=F32)
        return carry

    lax.fori_loop(0, zdev, across, 0, unroll=4)

    cen = [centers[j] for j in range(nb)]
    hei = [heights[j] for j in range(nb)]
    cur = []
    for j in range(nb):
        wid = jnp.full((rows_blk, ydev), widths[j], F32)
        cur.append((-0.5 * LOG2E) / (wid * wid))

    def block(row):
        here = pl.ds(pl.multiple_of(row, SUB), rows_blk)
        body = pl.ds(pl.multiple_of(row + SUB, SUB), rows_blk)
        above = pl.ds(row + SUB - 1, rows_blk)
        below = pl.ds(row + SUB + 1, rows_blk)
        fac = factor[here]

        def sample(z, carry):
            prev, val, depth, gone, sums = carry
            after = vf[z + 2, body]
            dz = after - prev
            dx = vf[z + 1, below] - vf[z + 1, above]
            dy = gy[z, here]
            facing = (0.7 * 0.64) * dz + (0.7 * 0.48) * dx + (0.7 * 0.6) * dy
            shade = 0.3 + jnp.abs(facing) * lax.rsqrt(dz * dz + dx * dx + dy * dy + 4.0)
            shade = shade.astype(BF16).astype(F32)
            bumps = []
            sigma = None
            for j in range(nb):
                off = val - cen[j]
                bump = jnp.exp2(off * cur[j] * off)
                bumps.append(bump)
                sigma = hei[j] * bump if sigma is None else sigma + hei[j] * bump
            depth = depth + sigma * fac
            now = jnp.exp2(depth)
            weight = (now - gone) * shade
            sums = tuple(acc + weight * bump for acc, bump in zip(sums, bumps))
            return val, after, depth, now, sums

        zero = jnp.zeros((rows_blk, ydev), F32)
        init = (vf[0, body], vf[1, body], zero, zero + 1.0, (zero,) * nb)
        _, _, depth, _, sums = lax.fori_loop(0, zdev, sample, init, unroll=4)
        mark = flag[here] > 0.5
        scale = jnp.where(mark, jnp.exp2(-depth), -1.0)
        logt = jnp.where(mark, -depth, depth) * (1.0 / LOG2E)
        chans = []
        for chan in range(3):
            total = None
            for j in range(nb):
                term = colours[j, chan] * sums[j]
                total = term if total is None else total + term
            chans.append(total * scale)
        return chans + [logt]

    def tile(owner, dest, slot):
        def one(i, carry):
            local = pl.multiple_of(i * rows_blk, SUB)
            values = block(owner * rows_out + local)
            for chan, value in enumerate(values):
                dest[slot, chan, pl.ds(local, rows_blk)] = value
            return carry

        lax.fori_loop(0, rows_out // rows_blk, one, 0)

    def send_of(owner):
        return pltpu.make_async_remote_copy(
            src_ref=tiles_out.at[owner], dst_ref=tiles_in.at[me], send_sem=tile_send.at[owner],
            recv_sem=tile_recv.at[me], device_id={"depth": owner}, device_id_type=MESH)

    def other(step, carry):
        owner = lax.rem(me + step, ndepth)
        tile(owner, tiles_out, owner)
        send_of(owner).start()
        return carry

    lax.fori_loop(1, ndepth, other, 0)
    tile(me, tiles_in, me)

    for step in range(1, ndepth):
        owner = lax.rem(me + step, ndepth)
        pltpu.make_async_remote_copy(
            src_ref=tiles_out.at[owner], dst_ref=tiles_in.at[owner], send_sem=tile_send.at[owner],
            recv_sem=tile_recv.at[owner], device_id={"depth": owner}, device_id_type=MESH).wait()

    mark = flag[pl.ds(pl.multiple_of(me * rows_out, SUB), rows_out)] > 0.5
    zero = jnp.zeros((rows_out, ydev), F32)
    done, through, total = [zero] * 3, zero + 1.0, zero
    for slab in range(ndepth):
        logt = tiles_in[slab, 3]
        clear = jnp.exp(logt)
        keep = jnp.where(mark, clear, 1.0)
        ahead = jnp.where(mark, 1.0, through)
        done = [keep * done[chan] + ahead * tiles_in[slab, chan] for chan in range(3)]
        through = through * clear
        total = total + logt
    for chan in range(3):
        colour_out[chan] = done[chan]
    logt_out[...] = total


def local(field, brick_live, order, centers, widths, heights, colours):
    counts = tuple(lax.axis_size(axis) for axis in ("depth", "imx", "imy"))
    zdev, xdev, ydev = field.shape
    ndepth = counts[0]
    rows_out = xdev // ndepth
    step_len = OPTICAL / (zdev * ndepth)
    vmem = pl.BlockSpec(memory_space=pltpu.VMEM)
    smem = pl.BlockSpec(memory_space=pltpu.SMEM)
    dma = pltpu.SemaphoreType.DMA
    return pl.pallas_call(
        functools.partial(kernel, counts, step_len),
        out_shape=(
            jax.ShapeDtypeStruct((3, rows_out, ydev), F32),
            jax.ShapeDtypeStruct((rows_out, ydev), F32),
        ),
        in_specs=[pl.BlockSpec(memory_space=pl.ANY), vmem, vmem, smem, smem, smem, smem],
        out_specs=(vmem, vmem),
        scratch_shapes=[
            pltpu.VMEM((zdev, xdev, ydev), BF16),
            pltpu.VMEM((zdev + 2, xdev + 2 * SUB, ydev), F32),
            pltpu.VMEM((xdev, ydev), BF16),
            pltpu.VMEM((xdev, ydev), BF16),
            pltpu.VMEM((zdev, PACK, ydev), BF16),
            pltpu.VMEM((zdev, PACK, ydev), BF16),
            pltpu.VMEM((xdev, LANES), BF16),
            pltpu.VMEM((xdev, LANES), BF16),
            pltpu.VMEM((xdev, LANES), BF16),
            pltpu.VMEM((zdev, xdev, ydev), F32),
            pltpu.VMEM((xdev, ydev), F32),
            pltpu.VMEM((xdev, ydev), F32),
            pltpu.VMEM((ndepth, 4, rows_out, ydev), F32),
            pltpu.VMEM((ndepth, 4, rows_out, ydev), F32),
            dma,
            dma((6,)),
            dma((6,)),
            dma((ndepth,)),
            dma((ndepth,)),
        ],
        compiler_params=pltpu.CompilerParams(collective_id=0, has_side_effects=True),
    )(field, brick_live, order, centers, widths, heights, colours)


def solution(mesh):
    return jax.shard_map(
        local,
        mesh=mesh,
        in_specs=(
            P("depth", "imy", "imx"),
            P("depth", "imy", "imx"),
            P("imy", "imx"),
            P(),
            P(),
            P(),
            P(),
        ),
        out_specs=(P(None, ("imy", "depth"), "imx"), P(("imy", "depth"), "imx")),
        check_vma=False,
    )
```

```python
import functools
import math

import jax
import jax.numpy as jnp
from jax import lax
from jax.experimental import pallas as pl
from jax.experimental.pallas import tpu as pltpu
from jax.sharding import PartitionSpec as P

OPTICAL = 3.0
MESH = pl.DeviceIdType.MESH
SUB = 8
PACK = 16
F32 = jnp.float32
BF16 = jnp.bfloat16
LOG2E = math.log2(math.e)


def iota(shape, dim):
    return lax.broadcasted_iota(jnp.int32, shape, dim)


def expand(small, rows, cols):
    high, wide = small.shape
    down = (iota((rows, high), 0) // (rows // high) == iota((rows, high), 1)).astype(F32).astype(BF16)
    along = (iota((wide, cols), 1) // (cols // wide) == iota((wide, cols), 0)).astype(F32).astype(BF16)
    tall = jnp.dot(down, small.astype(F32).astype(BF16), preferred_element_type=F32)
    return jnp.dot(tall.astype(BF16), along, preferred_element_type=F32)


def kernel(
    counts, step_len,
    field, live_in, order_in, centers_in, widths_in, heights_in, colours_in,
    colour_out, logt_out,
    fb, live, order, centers, widths, heights, colours,
    vf, zlo, zhi, xlo, xhi, face, flo, fhi, weights, lobes, scales, flag, logs, logs_in, tiles_out, tiles_in, edges,
    load_sem, halo_send, halo_recv, log_send, log_recv, tile_send, tile_recv,
):
    ndepth, nimx, nimy = counts
    me = lax.axis_index("depth")
    mx = lax.axis_index("imx")
    my = lax.axis_index("imy")
    zdev, xdev, ydev = fb.shape
    rows_out = xdev // ndepth
    nb = centers.shape[0]
    rows_blk = min(PACK, rows_out)

    pairs = ((field, fb), (order_in, order), (live_in, live), (centers_in, centers),
             (widths_in, widths), (heights_in, heights), (colours_in, colours))
    loads = [pltpu.make_async_copy(src, dst, load_sem.at[at]) for at, (src, dst) in enumerate(pairs)]
    for load in loads:
        load.start()

    barrier = pltpu.get_barrier_semaphore()
    for step in range(1, ndepth):
        pl.semaphore_signal(barrier, inc=1, device_id={"depth": lax.rem(me + step, ndepth)}, device_id_type=MESH)
    for axis, pos, count in (("imx", mx, nimx), ("imy", my, nimy)):
        @pl.when(pos > 0)
        def _():
            pl.semaphore_signal(barrier, inc=1, device_id={axis: pos - 1}, device_id_type=MESH)

        @pl.when(pos < count - 1)
        def _():
            pl.semaphore_signal(barrier, inc=1, device_id={axis: pos + 1}, device_id_type=MESH)

    for pos, count, low, high in ((me, ndepth, zlo, zhi), (mx, nimx, flo, fhi), (my, nimy, xlo, xhi)):
        @pl.when(pos == 0)
        def _():
            low[...] = jnp.zeros_like(low)

        @pl.when(pos == count - 1)
        def _():
            high[...] = jnp.zeros_like(high)

    peers = ndepth - 1
    for pos, count in ((mx, nimx), (my, nimy)):
        peers = peers + (pos + count - 1) // count + (2 * count - 2 - pos) // count
    pl.semaphore_wait(barrier, peers)
    loads[0].wait()

    def links(axis, pos, count, down_src, up_src, low, high, at):
        to_low = pltpu.make_async_remote_copy(
            src_ref=down_src, dst_ref=high, send_sem=halo_send.at[at], recv_sem=halo_recv.at[at],
            device_id={axis: lax.rem(pos + count - 1, count)}, device_id_type=MESH)
        to_high = pltpu.make_async_remote_copy(
            src_ref=up_src, dst_ref=low, send_sem=halo_send.at[at + 1], recv_sem=halo_recv.at[at + 1],
            device_id={axis: lax.rem(pos + 1, count)}, device_id_type=MESH)
        return pos, count, to_low, to_high

    def start(link):
        pos, count, to_low, to_high = link

        @pl.when(pos > 0)
        def _():
            to_low.start()

        @pl.when(pos < count - 1)
        def _():
            to_high.start()

    def finish(link):
        pos, count, to_low, to_high = link

        @pl.when(pos > 0)
        def _():
            to_low.wait_send()
            to_high.wait_recv()

        @pl.when(pos < count - 1)
        def _():
            to_high.wait_send()
            to_low.wait_recv()

    zlink = links("depth", me, ndepth, fb.at[0], fb.at[zdev - 1], zlo, zhi, 0)
    xlink = links("imy", my, nimy, fb.at[:, pl.ds(0, PACK)], fb.at[:, pl.ds(xdev - PACK, PACK)], xlo, xhi, 2)
    ylink = links("imx", mx, nimx, face, face, flo, fhi, 4)
    start(zlink)
    start(xlink)

    lane = iota((xdev, ydev), 1)

    def widen(z, packed):
        value = fb[z].astype(F32)
        vf[z + 1, SUB:SUB + xdev] = value
        return jnp.where(lane // 2 == z, pltpu.roll(value, 2 * z + 1, 1), packed)

    face[...] = lax.fori_loop(0, zdev, widen, jnp.zeros((xdev, ydev), F32), unroll=4).astype(BF16)
    start(ylink)

    for load in loads[1:]:
        load.wait()
    back = expand(order[...], xdev, ydev)
    factor = (2.0 * back - 1.0) * expand(live[0], xdev, ydev) * (step_len * LOG2E)
    flag[...] = back
    scales[...] = factor
    cen = [centers[j] for j in range(nb)]
    hei = [heights[j] for j in range(nb)]
    cur = []
    for j in range(nb):
        wid = jnp.full((rows_blk, ydev), widths[j], F32)
        cur.append((-0.5 * LOG2E) / (wid * wid))

    def absorb(i, carry):
        row = i * rows_blk
        here = pl.ds(pl.multiple_of(row, SUB), rows_blk)
        body = pl.ds(pl.multiple_of(row + SUB, SUB), rows_blk)
        fac = scales[here]

        def sample(z, carry):
            depth, gone = carry
            val = vf[z + 1, body]
            sigma = None
            for j in range(nb):
                off = val - cen[j]
                bump = jnp.exp2(off * cur[j] * off)
                lobes[j, z, here] = bump
                sigma = hei[j] * bump if sigma is None else sigma + hei[j] * bump
            depth = depth + sigma * fac
            now = jnp.exp2(depth)
            weights[z, here] = now - gone
            return depth, now

        zero = jnp.zeros((rows_blk, ydev), F32)
        depth, _ = lax.fori_loop(0, zdev, sample, (zero, zero + 1.0), unroll=4)
        mark = flag[here] > 0.5
        scales[here] = jnp.where(mark, jnp.exp2(-depth), -1.0)
        logs[here] = jnp.where(mark, -depth, depth) * (1.0 / LOG2E)
        return carry

    lax.fori_loop(0, xdev // rows_blk, absorb, 0)

    def log_copy(owner, source):
        return pltpu.make_async_remote_copy(
            src_ref=logs.at[pl.ds(pl.multiple_of(owner * rows_out, SUB), rows_out)], dst_ref=logs_in.at[source],
            send_sem=log_send.at[owner], recv_sem=log_recv.at[source], device_id={"depth": owner}, device_id_type=MESH)

    for step in range(1, ndepth):
        log_copy(lax.rem(me + step, ndepth), me).start()
    logs_in[me] = logs[pl.ds(pl.multiple_of(me * rows_out, SUB), rows_out)]
    finish(zlink)
    vf[0, SUB:SUB + xdev] = zlo[...].astype(F32)
    vf[zdev + 1, SUB:SUB + xdev] = zhi[...].astype(F32)
    finish(xlink)

    def widen_rows(z, carry):
        vf[z + 1, 0:SUB] = xlo[z].astype(F32)[PACK - SUB:]
        vf[z + 1, SUB + xdev:] = xhi[z].astype(F32)[:SUB]
        return carry

    lax.fori_loop(0, zdev, widen_rows, 0, unroll=4)
    finish(ylink)

    fromleft = pltpu.roll(flo[...].astype(F32), 1, 1)
    fromright = pltpu.roll(fhi[...].astype(F32), ydev - 1, 1)
    edges[...] = pltpu.roll(jnp.where(lane % 2 == 0, fromright, fromleft), ydev - 1, 1)
    spot = iota((rows_blk, ydev), 1)
    first, last = spot == 0, spot == ydev - 1

    def block(row):
        here = pl.ds(pl.multiple_of(row, SUB), rows_blk)
        body = pl.ds(pl.multiple_of(row + SUB, SUB), rows_blk)
        above = pl.ds(row + SUB - 1, rows_blk)
        below = pl.ds(row + SUB + 1, rows_blk)

        def sample(z, carry):
            prev, val, side, sums = carry
            after = vf[z + 2, body]
            dz = after - prev
            dx = vf[z + 1, below] - vf[z + 1, above]
            dy = jnp.where(last, side, pltpu.roll(val, ydev - 1, 1)) - jnp.where(first, side, pltpu.roll(val, 1, 1))
            facing = (0.7 * 0.64) * dz + (0.7 * 0.48) * dx + (0.7 * 0.6) * dy
            shade = 0.3 + jnp.abs(facing) * lax.rsqrt(dz * dz + dx * dx + dy * dy + 4.0)
            weight = weights[z, here] * shade.astype(BF16).astype(F32)
            sums = tuple(acc + weight * lobes[j, z, here] for j, acc in enumerate(sums))
            return val, after, pltpu.roll(side, ydev - 2, 1), sums

        zero = jnp.zeros((rows_blk, ydev), F32)
        init = (vf[0, body], vf[1, body], edges[here], (zero,) * nb)
        _, _, _, sums = lax.fori_loop(0, zdev, sample, init, unroll=4)
        scale = scales[here]
        chans = []
        for chan in range(3):
            total = None
            for j in range(nb):
                term = colours[j, chan] * sums[j]
                total = term if total is None else total + term
            chans.append(total * scale)
        return chans

    def tile(owner, dest, slot):
        def one(i, carry):
            local = pl.multiple_of(i * rows_blk, SUB)
            values = block(owner * rows_out + local)
            for chan, value in enumerate(values):
                dest[slot, chan, pl.ds(local, rows_blk)] = value
            return carry

        lax.fori_loop(0, rows_out // rows_blk, one, 0)

    def send_of(owner):
        return pltpu.make_async_remote_copy(
            src_ref=tiles_out.at[owner], dst_ref=tiles_in.at[me], send_sem=tile_send.at[owner],
            recv_sem=tile_recv.at[me], device_id={"depth": owner}, device_id_type=MESH)

    def other(step, carry):
        owner = lax.rem(me + step, ndepth)
        tile(owner, tiles_out, owner)
        send_of(owner).start()
        return carry

    lax.fori_loop(1, ndepth, other, 0)
    tile(me, tiles_in, me)

    for step in range(1, ndepth):
        owner = lax.rem(me + step, ndepth)
        pltpu.make_async_remote_copy(
            src_ref=tiles_out.at[owner], dst_ref=tiles_in.at[owner], send_sem=tile_send.at[owner],
            recv_sem=tile_recv.at[owner], device_id={"depth": owner}, device_id_type=MESH).wait()
        log_copy(owner, owner).wait()

    mark = flag[pl.ds(pl.multiple_of(me * rows_out, SUB), rows_out)] > 0.5
    zero = jnp.zeros((rows_out, ydev), F32)
    done, through, total = [zero] * 3, zero + 1.0, zero
    for slab in range(ndepth):
        logt = logs_in[slab]
        clear = jnp.exp(logt)
        keep = jnp.where(mark, clear, 1.0)
        ahead = jnp.where(mark, 1.0, through)
        done = [keep * done[chan] + ahead * tiles_in[slab, chan] for chan in range(3)]
        through = through * clear
        total = total + logt
    for chan in range(3):
        colour_out[chan] = done[chan]
    logt_out[...] = total


def local(field, brick_live, order, centers, widths, heights, colours):
    counts = tuple(lax.axis_size(axis) for axis in ("depth", "imx", "imy"))
    zdev, xdev, ydev = field.shape
    ndepth = counts[0]
    rows_out = xdev // ndepth
    step_len = OPTICAL / (zdev * ndepth)
    vmem = pl.BlockSpec(memory_space=pltpu.VMEM)
    dma = pltpu.SemaphoreType.DMA
    return pl.pallas_call(
        functools.partial(kernel, counts, step_len),
        out_shape=(
            pltpu.VMEM((3, rows_out, ydev), F32),
            pltpu.VMEM((rows_out, ydev), F32),
        ),
        in_specs=[pl.BlockSpec(memory_space=pl.ANY)] * 7,
        out_specs=(vmem, vmem),
        scratch_shapes=[
            pltpu.VMEM((zdev, xdev, ydev), BF16),
            pltpu.VMEM(brick_live.shape, jnp.int32),
            pltpu.VMEM(order.shape, jnp.int32),
            pltpu.SMEM(centers.shape, F32),
            pltpu.SMEM(widths.shape, F32),
            pltpu.SMEM(heights.shape, F32),
            pltpu.SMEM(colours.shape, F32),
            pltpu.VMEM((zdev + 2, xdev + 2 * SUB, ydev), F32),
            pltpu.VMEM((xdev, ydev), BF16),
            pltpu.VMEM((xdev, ydev), BF16),
            pltpu.VMEM((zdev, PACK, ydev), BF16),
            pltpu.VMEM((zdev, PACK, ydev), BF16),
            pltpu.VMEM((xdev, ydev), BF16),
            pltpu.VMEM((xdev, ydev), BF16),
            pltpu.VMEM((xdev, ydev), BF16),
            pltpu.VMEM((zdev, xdev, ydev), F32),
            pltpu.VMEM((centers.shape[0], zdev, xdev, ydev), F32),
            pltpu.VMEM((xdev, ydev), F32),
            pltpu.VMEM((xdev, ydev), F32),
            pltpu.VMEM((xdev, ydev), F32),
            pltpu.VMEM((ndepth, rows_out, ydev), F32),
            pltpu.VMEM((ndepth, 3, rows_out, ydev), F32),
            pltpu.VMEM((ndepth, 3, rows_out, ydev), F32),
            pltpu.VMEM((xdev, ydev), F32),
            dma((7,)),
            dma((6,)),
            dma((6,)),
            dma((ndepth,)),
            dma((ndepth,)),
            dma((ndepth,)),
            dma((ndepth,)),
        ],
        compiler_params=pltpu.CompilerParams(collective_id=0, has_side_effects=True),
    )(field, brick_live, order, centers, widths, heights, colours)


def solution(mesh):
    return jax.shard_map(
        local,
        mesh=mesh,
        in_specs=(
            P("depth", "imy", "imx"),
            P("depth", "imy", "imx"),
            P("imy", "imx"),
            P(),
            P(),
            P(),
            P(),
        ),
        out_specs=(P(None, ("imy", "depth"), "imx"), P(("imy", "depth"), "imx")),
        check_vma=False,
    )
```

```python
import functools
import math

import jax
import jax.numpy as jnp
from jax import lax
from jax.experimental import pallas as pl
from jax.experimental.pallas import tpu as pltpu
from jax.sharding import PartitionSpec as P

OPTICAL = 3.0
MESH = pl.DeviceIdType.MESH
SUB = 8
PACK = 16
F32 = jnp.float32
BF16 = jnp.bfloat16
LOG2E = math.log2(math.e)


def iota(shape, dim):
    return lax.broadcasted_iota(jnp.int32, shape, dim)


def expand(small, rows, cols):
    high, wide = small.shape
    down = (iota((rows, high), 0) // (rows // high) == iota((rows, high), 1)).astype(F32).astype(BF16)
    along = (iota((wide, cols), 1) // (cols // wide) == iota((wide, cols), 0)).astype(F32).astype(BF16)
    tall = jnp.dot(down, small.astype(F32).astype(BF16), preferred_element_type=F32)
    return jnp.dot(tall.astype(BF16), along, preferred_element_type=F32)


def kernel(
    counts, step_len,
    field, live_in, order_in, centers_in, widths_in, heights_in, colours_in,
    colour_out, logt_out,
    fb, live, order, centers, widths, heights, colours,
    vf, zlo, zhi, xlo, xhi, face, flo, fhi, weights, lobes, scales, flag, logs, logs_in, tiles_out, tiles_in, gy,
    load_sem, halo_send, halo_recv, log_send, log_recv, tile_send, tile_recv,
):
    ndepth, nimx, nimy = counts
    me = lax.axis_index("depth")
    mx = lax.axis_index("imx")
    my = lax.axis_index("imy")
    zdev, xdev, ydev = fb.shape
    rows_out = xdev // ndepth
    nb = centers.shape[0]
    rows_blk = min(PACK, rows_out)

    pairs = ((field, fb), (order_in, order), (live_in, live), (centers_in, centers),
             (widths_in, widths), (heights_in, heights), (colours_in, colours))
    loads = [pltpu.make_async_copy(src, dst, load_sem.at[at]) for at, (src, dst) in enumerate(pairs)]
    for load in loads:
        load.start()

    barrier = pltpu.get_barrier_semaphore()
    for step in range(1, ndepth):
        pl.semaphore_signal(barrier, inc=1, device_id={"depth": lax.rem(me + step, ndepth)}, device_id_type=MESH)
    for axis, pos, count in (("imx", mx, nimx), ("imy", my, nimy)):
        @pl.when(pos > 0)
        def _():
            pl.semaphore_signal(barrier, inc=1, device_id={axis: pos - 1}, device_id_type=MESH)

        @pl.when(pos < count - 1)
        def _():
            pl.semaphore_signal(barrier, inc=1, device_id={axis: pos + 1}, device_id_type=MESH)

    for pos, count, low, high in ((me, ndepth, zlo, zhi), (mx, nimx, flo, fhi), (my, nimy, xlo, xhi)):
        @pl.when(pos == 0)
        def _():
            low[...] = jnp.zeros_like(low)

        @pl.when(pos == count - 1)
        def _():
            high[...] = jnp.zeros_like(high)

    peers = ndepth - 1
    for pos, count in ((mx, nimx), (my, nimy)):
        peers = peers + (pos + count - 1) // count + (2 * count - 2 - pos) // count
    pl.semaphore_wait(barrier, peers)
    loads[0].wait()

    def links(axis, pos, count, down_src, up_src, low, high, at):
        to_low = pltpu.make_async_remote_copy(
            src_ref=down_src, dst_ref=high, send_sem=halo_send.at[at], recv_sem=halo_recv.at[at],
            device_id={axis: lax.rem(pos + count - 1, count)}, device_id_type=MESH)
        to_high = pltpu.make_async_remote_copy(
            src_ref=up_src, dst_ref=low, send_sem=halo_send.at[at + 1], recv_sem=halo_recv.at[at + 1],
            device_id={axis: lax.rem(pos + 1, count)}, device_id_type=MESH)
        return pos, count, to_low, to_high

    def start(link):
        pos, count, to_low, to_high = link

        @pl.when(pos > 0)
        def _():
            to_low.start()

        @pl.when(pos < count - 1)
        def _():
            to_high.start()

    def finish(link):
        pos, count, to_low, to_high = link

        @pl.when(pos > 0)
        def _():
            to_low.wait_send()
            to_high.wait_recv()

        @pl.when(pos < count - 1)
        def _():
            to_high.wait_send()
            to_low.wait_recv()

    zlink = links("depth", me, ndepth, fb.at[0], fb.at[zdev - 1], zlo, zhi, 0)
    xlink = links("imy", my, nimy, fb.at[:, pl.ds(0, PACK)], fb.at[:, pl.ds(xdev - PACK, PACK)], xlo, xhi, 2)
    ylink = links("imx", mx, nimx, face, face, flo, fhi, 4)
    start(zlink)
    start(xlink)

    lane = iota((xdev, ydev), 1)

    def widen(z, packed):
        value = fb[z].astype(F32)
        vf[z + 1, SUB:SUB + xdev] = value
        return jnp.where(lane // 2 == z, pltpu.roll(value, 2 * z + 1, 1), packed)

    face[...] = lax.fori_loop(0, zdev, widen, jnp.zeros((xdev, ydev), F32), unroll=8).astype(BF16)
    start(ylink)

    for load in loads[1:]:
        load.wait()
    back = expand(order[...], xdev, ydev)
    factor = (2.0 * back - 1.0) * expand(live[0], xdev, ydev) * (step_len * LOG2E)
    flag[...] = back
    scales[...] = factor
    cen = [centers[j] for j in range(nb)]
    hei = [heights[j] for j in range(nb)]
    cur = []
    for j in range(nb):
        wid = jnp.full((rows_blk, ydev), widths[j], F32)
        cur.append((-0.5 * LOG2E) / (wid * wid))

    def absorb(i, carry):
        row = i * rows_blk
        here = pl.ds(pl.multiple_of(row, SUB), rows_blk)
        body = pl.ds(pl.multiple_of(row + SUB, SUB), rows_blk)
        fac = scales[here]

        def sample(z, carry):
            depth, gone = carry
            val = vf[z + 1, body]
            sigma = None
            for j in range(nb):
                off = val - cen[j]
                bump = jnp.exp2(off * cur[j] * off)
                lobes[j, z, here] = bump
                sigma = hei[j] * bump if sigma is None else sigma + hei[j] * bump
            depth = depth + sigma * fac
            now = jnp.exp2(depth)
            weights[z, here] = now - gone
            return depth, now

        zero = jnp.zeros((rows_blk, ydev), F32)
        depth, _ = lax.fori_loop(0, zdev, sample, (zero, zero + 1.0), unroll=8)
        mark = flag[here] > 0.5
        scales[here] = jnp.where(mark, jnp.exp2(-depth), -1.0)
        logs[here] = jnp.where(mark, -depth, depth) * (1.0 / LOG2E)
        return carry

    lax.fori_loop(0, xdev // rows_blk, absorb, 0)

    def log_copy(owner, source):
        return pltpu.make_async_remote_copy(
            src_ref=logs.at[pl.ds(pl.multiple_of(owner * rows_out, SUB), rows_out)], dst_ref=logs_in.at[source],
            send_sem=log_send.at[owner], recv_sem=log_recv.at[source], device_id={"depth": owner}, device_id_type=MESH)

    for step in range(1, ndepth):
        log_copy(lax.rem(me + step, ndepth), me).start()
    logs_in[me] = logs[pl.ds(pl.multiple_of(me * rows_out, SUB), rows_out)]
    finish(zlink)
    vf[0, SUB:SUB + xdev] = zlo[...].astype(F32)
    vf[zdev + 1, SUB:SUB + xdev] = zhi[...].astype(F32)
    finish(xlink)

    def widen_rows(z, carry):
        vf[z + 1, 0:SUB] = xlo[z].astype(F32)[PACK - SUB:]
        vf[z + 1, SUB + xdev:] = xhi[z].astype(F32)[:SUB]
        return carry

    lax.fori_loop(0, zdev, widen_rows, 0, unroll=4)
    finish(ylink)

    fromleft = pltpu.roll(flo[...].astype(F32), 1, 1)
    fromright = pltpu.roll(fhi[...].astype(F32), ydev - 1, 1)
    edges = jnp.where(lane % 2 == 0, fromright, fromleft)
    k_at, l_at = iota((2 * ydev, ydev), 0), iota((2 * ydev, ydev), 1)
    odd = k_at % 2 == 1
    plus = (k_at < ydev) & (k_at == l_at + 1) | (k_at >= ydev) & (l_at == ydev - 1) & jnp.logical_not(odd)
    minus = (k_at < ydev) & (k_at == l_at - 1) | (k_at >= ydev) & (l_at == 0) & odd
    slope = (plus.astype(F32) - minus.astype(F32)).astype(BF16)

    def across(z, carry):
        side = jnp.where(lane // 2 == z, edges, 0.0).astype(BF16)
        gy[z] = jnp.dot(jnp.concatenate([fb[z], side], axis=1), slope, preferred_element_type=F32)
        return carry

    lax.fori_loop(0, zdev, across, 0, unroll=16)

    def block(row):
        here = pl.ds(pl.multiple_of(row, SUB), rows_blk)
        body = pl.ds(pl.multiple_of(row + SUB, SUB), rows_blk)
        above = pl.ds(row + SUB - 1, rows_blk)
        below = pl.ds(row + SUB + 1, rows_blk)

        def sample(z, carry):
            prev, val, sums = carry
            after = vf[z + 2, body]
            dz = after - prev
            dx = vf[z + 1, below] - vf[z + 1, above]
            dy = gy[z, here]
            facing = (0.7 * 0.64) * dz + (0.7 * 0.48) * dx + (0.7 * 0.6) * dy
            shade = 0.3 + jnp.abs(facing) * lax.rsqrt(dz * dz + dx * dx + dy * dy + 4.0)
            weight = weights[z, here] * shade.astype(BF16).astype(F32)
            sums = tuple(acc + weight * lobes[j, z, here] for j, acc in enumerate(sums))
            return val, after, sums

        zero = jnp.zeros((rows_blk, ydev), F32)
        init = (vf[0, body], vf[1, body], (zero,) * nb)
        _, _, sums = lax.fori_loop(0, zdev, sample, init, unroll=8)
        scale = scales[here]
        chans = []
        for chan in range(3):
            total = None
            for j in range(nb):
                term = colours[j, chan] * sums[j]
                total = term if total is None else total + term
            chans.append(total * scale)
        return chans

    def tile(owner, dest, slot):
        def one(i, carry):
            local = pl.multiple_of(i * rows_blk, SUB)
            values = block(owner * rows_out + local)
            for chan, value in enumerate(values):
                dest[slot, chan, pl.ds(local, rows_blk)] = value
            return carry

        lax.fori_loop(0, rows_out // rows_blk, one, 0)

    def send_of(owner):
        return pltpu.make_async_remote_copy(
            src_ref=tiles_out.at[owner], dst_ref=tiles_in.at[me], send_sem=tile_send.at[owner],
            recv_sem=tile_recv.at[me], device_id={"depth": owner}, device_id_type=MESH)

    def other(step, carry):
        owner = lax.rem(me + step, ndepth)
        tile(owner, tiles_out, owner)
        send_of(owner).start()
        return carry

    lax.fori_loop(1, ndepth, other, 0)
    tile(me, tiles_in, me)

    for step in range(1, ndepth):
        owner = lax.rem(me + step, ndepth)
        pltpu.make_async_remote_copy(
            src_ref=tiles_out.at[owner], dst_ref=tiles_in.at[owner], send_sem=tile_send.at[owner],
            recv_sem=tile_recv.at[owner], device_id={"depth": owner}, device_id_type=MESH).wait()
        log_copy(owner, owner).wait()

    mark = flag[pl.ds(pl.multiple_of(me * rows_out, SUB), rows_out)] > 0.5
    zero = jnp.zeros((rows_out, ydev), F32)
    done, through, total = [zero] * 3, zero + 1.0, zero
    for slab in range(ndepth):
        logt = logs_in[slab]
        clear = jnp.exp(logt)
        keep = jnp.where(mark, clear, 1.0)
        ahead = jnp.where(mark, 1.0, through)
        done = [keep * done[chan] + ahead * tiles_in[slab, chan] for chan in range(3)]
        through = through * clear
        total = total + logt
    for chan in range(3):
        colour_out[chan] = done[chan]
    logt_out[...] = total


def local(field, brick_live, order, centers, widths, heights, colours):
    counts = tuple(lax.axis_size(axis) for axis in ("depth", "imx", "imy"))
    zdev, xdev, ydev = field.shape
    ndepth = counts[0]
    rows_out = xdev // ndepth
    step_len = OPTICAL / (zdev * ndepth)
    vmem = pl.BlockSpec(memory_space=pltpu.VMEM)
    dma = pltpu.SemaphoreType.DMA
    return pl.pallas_call(
        functools.partial(kernel, counts, step_len),
        out_shape=(
            pltpu.VMEM((3, rows_out, ydev), F32),
            pltpu.VMEM((rows_out, ydev), F32),
        ),
        in_specs=[pl.BlockSpec(memory_space=pl.ANY)] * 7,
        out_specs=(vmem, vmem),
        scratch_shapes=[
            pltpu.VMEM((zdev, xdev, ydev), BF16),
            pltpu.VMEM(brick_live.shape, jnp.int32),
            pltpu.VMEM(order.shape, jnp.int32),
            pltpu.SMEM(centers.shape, F32),
            pltpu.SMEM(widths.shape, F32),
            pltpu.SMEM(heights.shape, F32),
            pltpu.SMEM(colours.shape, F32),
            pltpu.VMEM((zdev + 2, xdev + 2 * SUB, ydev), F32),
            pltpu.VMEM((xdev, ydev), BF16),
            pltpu.VMEM((xdev, ydev), BF16),
            pltpu.VMEM((zdev, PACK, ydev), BF16),
            pltpu.VMEM((zdev, PACK, ydev), BF16),
            pltpu.VMEM((xdev, ydev), BF16),
            pltpu.VMEM((xdev, ydev), BF16),
            pltpu.VMEM((xdev, ydev), BF16),
            pltpu.VMEM((zdev, xdev, ydev), F32),
            pltpu.VMEM((centers.shape[0], zdev, xdev, ydev), F32),
            pltpu.VMEM((xdev, ydev), F32),
            pltpu.VMEM((xdev, ydev), F32),
            pltpu.VMEM((xdev, ydev), F32),
            pltpu.VMEM((ndepth, rows_out, ydev), F32),
            pltpu.VMEM((ndepth, 3, rows_out, ydev), F32),
            pltpu.VMEM((ndepth, 3, rows_out, ydev), F32),
            pltpu.VMEM((zdev, xdev, ydev), F32),
            dma((7,)),
            dma((6,)),
            dma((6,)),
            dma((ndepth,)),
            dma((ndepth,)),
            dma((ndepth,)),
            dma((ndepth,)),
        ],
        compiler_params=pltpu.CompilerParams(collective_id=0, has_side_effects=True),
    )(field, brick_live, order, centers, widths, heights, colours)


def solution(mesh):
    return jax.shard_map(
        local,
        mesh=mesh,
        in_specs=(
            P("depth", "imy", "imx"),
            P("depth", "imy", "imx"),
            P("imy", "imx"),
            P(),
            P(),
            P(),
            P(),
        ),
        out_specs=(P(None, ("imy", "depth"), "imx"), P(("imy", "depth"), "imx")),
        check_vma=False,
    )
```

```python
import functools
import math

import jax
import jax.numpy as jnp
from jax import lax
from jax.experimental import pallas as pl
from jax.experimental.pallas import tpu as pltpu
from jax.sharding import PartitionSpec as P

OPTICAL = 3.0
MESH = pl.DeviceIdType.MESH
SUB = 8
PACK = 16
F32 = jnp.float32
BF16 = jnp.bfloat16
LEVELS = 32000.0
LOG2E = math.log2(math.e)


def iota(shape, dim):
    return lax.broadcasted_iota(jnp.int32, shape, dim)


def expand(small, rows, cols):
    high, wide = small.shape
    down = (iota((rows, high), 0) // (rows // high) == iota((rows, high), 1)).astype(F32).astype(BF16)
    along = (iota((wide, cols), 1) // (cols // wide) == iota((wide, cols), 0)).astype(F32).astype(BF16)
    tall = jnp.dot(down, small.astype(F32).astype(BF16), preferred_element_type=F32)
    return jnp.dot(tall.astype(BF16), along, preferred_element_type=F32)


def kernel(
    counts, step_len,
    field, live_in, order_in, centers_in, widths_in, heights_in, colours_in,
    colour_out, logt_out,
    fb, live, order, centers, widths, heights, colours,
    vf, zlo, zhi, xlo, xhi, face, flo, fhi, weights, lobes, scales, flag, logs, logs_in, tiles_out, tiles_in, gy, stage, peaks_out, peaks_in,
    load_sem, halo_send, halo_recv, log_send, log_recv, tile_send, tile_recv, peak_send, peak_recv,
):
    ndepth, nimx, nimy = counts
    me = lax.axis_index("depth")
    mx = lax.axis_index("imx")
    my = lax.axis_index("imy")
    zdev, xdev, ydev = fb.shape
    rows_out = xdev // ndepth
    nb = centers.shape[0]
    rows_blk = min(PACK, rows_out)

    pairs = ((field, fb), (order_in, order), (live_in, live), (centers_in, centers),
             (widths_in, widths), (heights_in, heights), (colours_in, colours))
    loads = [pltpu.make_async_copy(src, dst, load_sem.at[at]) for at, (src, dst) in enumerate(pairs)]
    for load in loads:
        load.start()

    barrier = pltpu.get_barrier_semaphore()
    for step in range(1, ndepth):
        pl.semaphore_signal(barrier, inc=1, device_id={"depth": lax.rem(me + step, ndepth)}, device_id_type=MESH)
    for axis, pos, count in (("imx", mx, nimx), ("imy", my, nimy)):
        @pl.when(pos > 0)
        def _():
            pl.semaphore_signal(barrier, inc=1, device_id={axis: pos - 1}, device_id_type=MESH)

        @pl.when(pos < count - 1)
        def _():
            pl.semaphore_signal(barrier, inc=1, device_id={axis: pos + 1}, device_id_type=MESH)

    for pos, count, low, high in ((me, ndepth, zlo, zhi), (mx, nimx, flo, fhi), (my, nimy, xlo, xhi)):
        @pl.when(pos == 0)
        def _():
            low[...] = jnp.zeros_like(low)

        @pl.when(pos == count - 1)
        def _():
            high[...] = jnp.zeros_like(high)

    peers = ndepth - 1
    for pos, count in ((mx, nimx), (my, nimy)):
        peers = peers + (pos + count - 1) // count + (2 * count - 2 - pos) // count
    pl.semaphore_wait(barrier, peers)
    loads[0].wait()

    def links(axis, pos, count, down_src, up_src, low, high, at):
        to_low = pltpu.make_async_remote_copy(
            src_ref=down_src, dst_ref=high, send_sem=halo_send.at[at], recv_sem=halo_recv.at[at],
            device_id={axis: lax.rem(pos + count - 1, count)}, device_id_type=MESH)
        to_high = pltpu.make_async_remote_copy(
            src_ref=up_src, dst_ref=low, send_sem=halo_send.at[at + 1], recv_sem=halo_recv.at[at + 1],
            device_id={axis: lax.rem(pos + 1, count)}, device_id_type=MESH)
        return pos, count, to_low, to_high

    def start(link):
        pos, count, to_low, to_high = link

        @pl.when(pos > 0)
        def _():
            to_low.start()

        @pl.when(pos < count - 1)
        def _():
            to_high.start()

    def finish(link):
        pos, count, to_low, to_high = link

        @pl.when(pos > 0)
        def _():
            to_low.wait_send()
            to_high.wait_recv()

        @pl.when(pos < count - 1)
        def _():
            to_high.wait_send()
            to_low.wait_recv()

    zlink = links("depth", me, ndepth, fb.at[0], fb.at[zdev - 1], zlo, zhi, 0)
    xlink = links("imy", my, nimy, fb.at[:, pl.ds(0, PACK)], fb.at[:, pl.ds(xdev - PACK, PACK)], xlo, xhi, 2)
    ylink = links("imx", mx, nimx, face, face, flo, fhi, 4)
    start(zlink)
    start(xlink)

    lane = iota((xdev, ydev), 1)

    def widen(z, packed):
        value = fb[z].astype(F32)
        vf[z + 1, SUB:SUB + xdev] = value
        return jnp.where(lane // 2 == z, pltpu.roll(value, 2 * z + 1, 1), packed)

    face[...] = lax.fori_loop(0, zdev, widen, jnp.zeros((xdev, ydev), F32), unroll=8).astype(BF16)
    start(ylink)

    for load in loads[1:]:
        load.wait()
    back = expand(order[...], xdev, ydev)
    factor = (2.0 * back - 1.0) * expand(live[0], xdev, ydev) * (step_len * LOG2E)
    flag[...] = back
    scales[...] = factor
    cen = [centers[j] for j in range(nb)]
    hei = [heights[j] for j in range(nb)]
    cur = []
    for j in range(nb):
        wid = jnp.full((rows_blk, ydev), widths[j], F32)
        cur.append((-0.5 * LOG2E) / (wid * wid))

    def absorb(i, carry):
        row = i * rows_blk
        here = pl.ds(pl.multiple_of(row, SUB), rows_blk)
        body = pl.ds(pl.multiple_of(row + SUB, SUB), rows_blk)
        fac = scales[here]

        def sample(z, carry):
            depth, gone = carry
            val = vf[z + 1, body]
            sigma = None
            for j in range(nb):
                off = val - cen[j]
                bump = jnp.exp2(off * cur[j] * off)
                lobes[j, z, here] = bump
                sigma = hei[j] * bump if sigma is None else sigma + hei[j] * bump
            depth = depth + sigma * fac
            now = jnp.exp2(depth)
            weights[z, here] = now - gone
            return depth, now

        zero = jnp.zeros((rows_blk, ydev), F32)
        depth, _ = lax.fori_loop(0, zdev, sample, (zero, zero + 1.0), unroll=8)
        mark = flag[here] > 0.5
        scales[here] = jnp.where(mark, jnp.exp2(-depth), -1.0)
        logs[here] = jnp.where(mark, -depth, depth) * (1.0 / LOG2E)
        return carry

    lax.fori_loop(0, xdev // rows_blk, absorb, 0)

    def log_copy(owner, source):
        return pltpu.make_async_remote_copy(
            src_ref=logs.at[pl.ds(pl.multiple_of(owner * rows_out, SUB), rows_out)], dst_ref=logs_in.at[source],
            send_sem=log_send.at[owner], recv_sem=log_recv.at[source], device_id={"depth": owner}, device_id_type=MESH)

    for step in range(1, ndepth):
        log_copy(lax.rem(me + step, ndepth), me).start()
    logs_in[me] = logs[pl.ds(pl.multiple_of(me * rows_out, SUB), rows_out)]
    finish(zlink)
    vf[0, SUB:SUB + xdev] = zlo[...].astype(F32)
    vf[zdev + 1, SUB:SUB + xdev] = zhi[...].astype(F32)
    finish(xlink)

    def widen_rows(z, carry):
        vf[z + 1, 0:SUB] = xlo[z].astype(F32)[PACK - SUB:]
        vf[z + 1, SUB + xdev:] = xhi[z].astype(F32)[:SUB]
        return carry

    lax.fori_loop(0, zdev, widen_rows, 0, unroll=4)
    finish(ylink)

    fromleft = pltpu.roll(flo[...].astype(F32), 1, 1)
    fromright = pltpu.roll(fhi[...].astype(F32), ydev - 1, 1)
    edges = jnp.where(lane % 2 == 0, fromright, fromleft)
    k_at, l_at = iota((2 * ydev, ydev), 0), iota((2 * ydev, ydev), 1)
    odd = k_at % 2 == 1
    plus = (k_at < ydev) & (k_at == l_at + 1) | (k_at >= ydev) & (l_at == ydev - 1) & jnp.logical_not(odd)
    minus = (k_at < ydev) & (k_at == l_at - 1) | (k_at >= ydev) & (l_at == 0) & odd
    slope = (plus.astype(F32) - minus.astype(F32)).astype(BF16)

    def across(z, carry):
        side = jnp.where(lane // 2 == z, edges, 0.0).astype(BF16)
        gy[z] = jnp.dot(jnp.concatenate([fb[z], side], axis=1), slope, preferred_element_type=F32)
        return carry

    lax.fori_loop(0, zdev, across, 0, unroll=16)

    def block(row):
        here = pl.ds(pl.multiple_of(row, SUB), rows_blk)
        body = pl.ds(pl.multiple_of(row + SUB, SUB), rows_blk)
        above = pl.ds(row + SUB - 1, rows_blk)
        below = pl.ds(row + SUB + 1, rows_blk)

        def sample(z, carry):
            prev, val, sums = carry
            after = vf[z + 2, body]
            dz = after - prev
            dx = vf[z + 1, below] - vf[z + 1, above]
            dy = gy[z, here]
            facing = (0.7 * 0.64) * dz + (0.7 * 0.48) * dx + (0.7 * 0.6) * dy
            shade = 0.3 + jnp.abs(facing) * lax.rsqrt(dz * dz + dx * dx + dy * dy + 4.0)
            weight = weights[z, here] * shade.astype(BF16).astype(F32)
            sums = tuple(acc + weight * lobes[j, z, here] for j, acc in enumerate(sums))
            return val, after, sums

        zero = jnp.zeros((rows_blk, ydev), F32)
        init = (vf[0, body], vf[1, body], (zero,) * nb)
        _, _, sums = lax.fori_loop(0, zdev, sample, init, unroll=8)
        scale = scales[here]
        chans = []
        for chan in range(3):
            total = None
            for j in range(nb):
                term = colours[j, chan] * sums[j]
                total = term if total is None else total + term
            chans.append(total * scale)
        return chans

    def tile(owner):
        def one(i, carry):
            local = pl.multiple_of(i * rows_blk, SUB)
            values = block(owner * rows_out + local)
            for chan, value in enumerate(values):
                stage[chan, pl.ds(local, rows_blk)] = value
            return carry

        lax.fori_loop(0, rows_out // rows_blk, one, 0)

    def sends(owner, source):
        place = {"depth": owner}
        return (
            pltpu.make_async_remote_copy(
                src_ref=tiles_out.at[owner], dst_ref=tiles_in.at[source], send_sem=tile_send.at[owner],
                recv_sem=tile_recv.at[source], device_id=place, device_id_type=MESH),
            pltpu.make_async_remote_copy(
                src_ref=peaks_out.at[owner], dst_ref=peaks_in.at[source], send_sem=peak_send.at[owner],
                recv_sem=peak_recv.at[source], device_id=place, device_id_type=MESH),
        )

    tiles_in[me] = jnp.zeros((3, rows_out, ydev), jnp.int16)
    peaks_in[me] = jnp.zeros((SUB, ydev), F32)

    def other(step, carry):
        owner = lax.rem(me + step, ndepth)
        tile(owner)
        line = iota((SUB, ydev), 0)
        peaks = jnp.zeros((SUB, ydev), F32)
        for chan in range(3):
            value = stage[chan]
            peak = jnp.maximum(jnp.max(value, axis=0, keepdims=True), 1e-30)
            peaks = jnp.where(line == chan, peak * (1.0 / LEVELS), peaks)
            tiles_out[owner, chan] = (value * (LEVELS / peak) + 0.5).astype(jnp.int32).astype(jnp.int16)
        peaks_out[owner] = peaks
        for copy in sends(owner, me):
            copy.start()
        return carry

    lax.fori_loop(1, ndepth, other, 0)
    tile(me)

    for step in range(1, ndepth):
        owner = lax.rem(me + step, ndepth)
        for copy in sends(owner, owner):
            copy.wait()
        log_copy(owner, owner).wait()

    mark = flag[pl.ds(pl.multiple_of(me * rows_out, SUB), rows_out)] > 0.5
    zero = jnp.zeros((rows_out, ydev), F32)
    done, through, total = [zero] * 3, zero + 1.0, zero
    for slab in range(ndepth):
        logt = logs_in[slab]
        clear = jnp.exp(logt)
        keep = jnp.where(mark, clear, 1.0)
        ahead = jnp.where(mark, 1.0, through)
        for chan in range(3):
            value = tiles_in[slab, chan].astype(jnp.int32).astype(F32) * peaks_in[slab, chan:chan + 1]
            value = jnp.where(me == slab, stage[chan], value)
            done[chan] = keep * done[chan] + ahead * value
        through = through * clear
        total = total + logt
    for chan in range(3):
        colour_out[chan] = done[chan]
    logt_out[...] = total


def local(field, brick_live, order, centers, widths, heights, colours):
    counts = tuple(lax.axis_size(axis) for axis in ("depth", "imx", "imy"))
    zdev, xdev, ydev = field.shape
    ndepth = counts[0]
    rows_out = xdev // ndepth
    step_len = OPTICAL / (zdev * ndepth)
    vmem = pl.BlockSpec(memory_space=pltpu.VMEM)
    dma = pltpu.SemaphoreType.DMA
    return pl.pallas_call(
        functools.partial(kernel, counts, step_len),
        out_shape=(
            pltpu.VMEM((3, rows_out, ydev), F32),
            pltpu.VMEM((rows_out, ydev), F32),
        ),
        in_specs=[pl.BlockSpec(memory_space=pl.ANY)] * 7,
        out_specs=(vmem, vmem),
        scratch_shapes=[
            pltpu.VMEM((zdev, xdev, ydev), BF16),
            pltpu.VMEM(brick_live.shape, jnp.int32),
            pltpu.VMEM(order.shape, jnp.int32),
            pltpu.SMEM(centers.shape, F32),
            pltpu.SMEM(widths.shape, F32),
            pltpu.SMEM(heights.shape, F32),
            pltpu.SMEM(colours.shape, F32),
            pltpu.VMEM((zdev + 2, xdev + 2 * SUB, ydev), F32),
            pltpu.VMEM((xdev, ydev), BF16),
            pltpu.VMEM((xdev, ydev), BF16),
            pltpu.VMEM((zdev, PACK, ydev), BF16),
            pltpu.VMEM((zdev, PACK, ydev), BF16),
            pltpu.VMEM((xdev, ydev), BF16),
            pltpu.VMEM((xdev, ydev), BF16),
            pltpu.VMEM((xdev, ydev), BF16),
            pltpu.VMEM((zdev, xdev, ydev), F32),
            pltpu.VMEM((centers.shape[0], zdev, xdev, ydev), F32),
            pltpu.VMEM((xdev, ydev), F32),
            pltpu.VMEM((xdev, ydev), F32),
            pltpu.VMEM((xdev, ydev), F32),
            pltpu.VMEM((ndepth, rows_out, ydev), F32),
            pltpu.VMEM((ndepth, 3, rows_out, ydev), jnp.int16),
            pltpu.VMEM((ndepth, 3, rows_out, ydev), jnp.int16),
            pltpu.VMEM((zdev, xdev, ydev), F32),
            pltpu.VMEM((3, rows_out, ydev), F32),
            pltpu.VMEM((ndepth, SUB, ydev), F32),
            pltpu.VMEM((ndepth, SUB, ydev), F32),
            dma((7,)),
            dma((6,)),
            dma((6,)),
            dma((ndepth,)),
            dma((ndepth,)),
            dma((ndepth,)),
            dma((ndepth,)),
            dma((ndepth,)),
            dma((ndepth,)),
        ],
        compiler_params=pltpu.CompilerParams(collective_id=0, has_side_effects=True),
    )(field, brick_live, order, centers, widths, heights, colours)


def solution(mesh):
    return jax.shard_map(
        local,
        mesh=mesh,
        in_specs=(
            P("depth", "imy", "imx"),
            P("depth", "imy", "imx"),
            P("imy", "imx"),
            P(),
            P(),
            P(),
            P(),
        ),
        out_specs=(P(None, ("imy", "depth"), "imx"), P(("imy", "depth"), "imx")),
        check_vma=False,
    )
```
